512 devices in a mesh: island: 64 (over z, y), tensor: 8 (over x, core).
Axes of the slice: x: 4, y: 4, z: 16, core: 2. Of those that a mesh axis runs over, the one named last changes fastest.
Arguments:
- pseudo_grad: float32 [64, 128, 53248], P('island', None, 'tensor'), may hold values from -8000 to 8000
- outer_params: float32 [128, 53248], P('island', 'tensor'), may hold values from -4 to 4
- momentum: float32 [128, 53248], P('island', 'tensor'), may hold values from -6 to 6
- save_pages: int32 [64], replicated, may hold values from 1 to 208, 6656 in all
- writer: int32 [64], replicated, may hold values from 0 to 63, each once
Outputs:
- new_master: float32 [128, 53248], P('island', 'tensor')
- new_momentum: float32 [128, 53248], P('island', 'tensor')
- checkpoint: bfloat16 [64, 208, 1024], P('island', None, 'tensor')
The draws below stay inside these ranges and needn't reach their ends.
Inputs may be any that keep to these rules, and one draw needn't show every extreme that they name: save_pages sums to 6656; the longest range has exactly 208 pages. writer names every island once.
All inputs are finite; a program needn't handle non-finite values.
Results may differ from the reference program's by a relative error of at most 0.0007.
Values may be sent and summed in bfloat16 or wider, within the bound.
No kernel may reach another device: no remote copies, remote signals or barrier semaphores. Data moves between devices by JAX's collectives and lax.ppermute only.
A program may use at most 64 MiB of HBM per device.

```python
import math
import jax
import jax.numpy as jnp
import numpy as np
from jax import lax

FF = 53248
ISLANDS = 64
ROWS = 128
PAGES = 6656
CAP = 208
N_TENSOR = 8


def draw_pseudo_grad(key, part):
    keys = jax.random.split(jax.random.fold_in(key, 17), 3)
    base = jax.random.truncated_normal(keys[0], -6.0, 6.0, (ISLANDS, ROWS, FF), jnp.float32)
    row_scale = jnp.exp(jax.random.uniform(keys[1], (ROWS,), jnp.float32, 0.0, math.log(10.0)))
    row_scale = row_scale * jnp.exp(math.log(3.0) * jnp.arange(ROWS, dtype=jnp.float32) / ROWS)
    col_scale = jnp.exp(jax.random.uniform(keys[2], (FF,), jnp.float32, 0.0, math.log(10.0)))
    col_scale = col_scale * jnp.exp(math.log(3.0) * jnp.arange(FF, dtype=jnp.float32) / FF)
    return base * row_scale[None, :, None] * col_scale[None, None, :]


def block_scale(key, dims, cuts, low, top_value):
    gain, own = 1.0, jax.random.fold_in(key, 6)
    for dim, blocks in cuts:
        steps = jnp.exp(jax.random.uniform(jax.random.fold_in(own, dim), (blocks,), jnp.float32, low / len(cuts), top_value / len(cuts)))
        gain = gain * jnp.repeat(steps, dims[dim] // blocks).reshape([-1 if axis == dim else 1 for axis in range(len(dims))])
    return gain


def profile(amount, total, most, lean):
    portions = [(1 << 20) // math.isqrt(grade ** lean) + 1 for grade in range(2, amount + 1)]
    surplus, given = total - most - (amount - 1), [1] * (amount - 1)
    while surplus > 0:
        candidates = [i for i in range(amount - 1) if given[i] < most]
        whole, remaining = sum([portions[i] for i in candidates]), surplus
        for i in candidates:
            more = min(most - given[i], max(1, remaining * portions[i] // whole), surplus)
            given[i] = given[i] + more
            surplus = surplus - more
    return np.array([most] + given)


def ragged(rng, amount, total, reach, slope):
    if amount == 2:
        one = jax.random.randint(rng, (), max(1, total - reach), min(reach, total - 1) + 1)
        return jnp.stack([one, total - one])
    tallies = jnp.asarray(profile(amount, total, reach, slope), jnp.int32)
    couples = (amount - 1) // 2
    source_of, receiver = tallies[1:1 + 2 * couples:2], tallies[2:2 + 2 * couples:2]
    margin = jnp.minimum(source_of - 1, reach - receiver)
    passed = jax.random.randint(jax.random.fold_in(rng, 1), (couples,), 0, 1 << 20) % (margin + 1)
    tallies = tallies.at[1:1 + 2 * couples:2].set(source_of - passed).at[2:2 + 2 * couples:2].set(receiver + passed)
    return tallies[jax.random.permutation(jax.random.fold_in(rng, 2), amount)]


def noise(stream_key, dims, width, bound, cuts=(), kind=jnp.bfloat16):
    array = jax.random.normal(stream_key, dims, jnp.float32) * width
    if len(cuts) > 0:
        array = block_scale(stream_key, dims, cuts, -0.22, 0.18) * array
    return jnp.clip(array, min=-bound, max=bound).astype(kind)


def setup_inputs(seed: int = 0) -> dict:
    key_of = jax.random.split(jax.random.key(seed), 6)
    return {
        "pseudo_grad": draw_pseudo_grad(jax.random.fold_in(key_of[5], 71), 0),
        "outer_params": noise(key_of[1], (ROWS, FF), 0.5, 4.0, ((0, 64), (1, 8)), jnp.float32),
        "momentum": noise(key_of[2], (ROWS, FF), 1.0, 6.0, ((0, 64), (1, 8)), jnp.float32),
        "save_pages": ragged(key_of[3], ISLANDS, PAGES, CAP, 2).astype(jnp.int32),
        "writer": jax.random.permutation(key_of[4], ISLANDS).astype(jnp.int32),
    }


epsilon = 1e-06
decay_rate = 0.9
outer_rate = 0.7

def reference(pseudo_grad, outer_params, momentum, save_pages, writer):

    def add_island(island_id, running):
        return running + pseudo_grad[island_id]
    summed = lax.fori_loop(0, ISLANDS, add_island, jnp.zeros((ROWS, FF), jnp.float32))
    outer_grad = summed / ISLANDS
    square_sum = jnp.sum(outer_grad * outer_grad)
    normed = outer_grad / jnp.sqrt(square_sum / (ROWS * FF) + epsilon)
    new_momentum = decay_rate * momentum + normed
    new_master = outer_params - outer_rate * (normed + decay_rate * new_momentum)
    cast_rows = new_master.astype(jnp.bfloat16)
    shards = FF // N_TENSOR
    page_table = cast_rows.reshape(ROWS, N_TENSOR, shards).transpose(1, 0, 2).reshape(N_TENSOR, PAGES, 128)
    starts = jnp.cumsum(save_pages).astype(jnp.int32) - save_pages
    ranges = jnp.arange(ISLANDS, dtype=jnp.int32)
    inverse = jnp.zeros((ISLANDS,), jnp.int32).at[writer].set(ranges)
    slot_ids = jnp.arange(CAP, dtype=jnp.int32)
    page_index = starts[inverse][:, None] + slot_ids[None, :]
    is_valid = slot_ids[None, :] < save_pages[inverse][:, None]
    page_index = jnp.clip(page_index, 0, PAGES - 1).astype(jnp.int32)
    picked = page_table[:, page_index]
    picked = jnp.where(is_valid[None, :, :, None], picked, jnp.zeros_like(picked))
    checkpoint = picked.transpose(1, 2, 0, 3).reshape(ISLANDS, CAP, N_TENSOR * 128)
    return (new_master, new_momentum, checkpoint)
```

```python
import jax
import jax.numpy as jnp
from jax import lax
from jax.sharding import Mesh
from jax.sharding import PartitionSpec as P

ISLAND = ("z", "y")
TENSOR = ("x", "core")

epsilon = 1e-06
decay_rate = 0.9
outer_rate = 0.7

NZ, NY, ROW_TILES, GROUPS, LANES = 16, 4, 16, 13, 128
PER_ROW = NY * GROUPS


def shift(n, by):
    return [(i, (i + by) % n) for i in range(n)]


def pick(array, index, axis_size):
    return lax.dynamic_index_in_dim(array, index % axis_size, 0, keepdims=False)


def summed_around(classes, axis, n):
    here = lax.axis_index(axis)
    half = classes.shape[1] // 2
    up, down = shift(n, 1), shift(n, -1)
    far = pick(classes, here + 2, 4)
    passed_up = lax.ppermute(far[:half], axis, up)
    passed_down = lax.ppermute(far[half:], axis, down)
    above, below, own = pick(classes, here + 1, 4), pick(classes, here + 3, 4), pick(classes, here, 4)
    near_up = lax.ppermute(above[half:], axis, up)
    near_down = lax.ppermute(below[:half], axis, down)
    joined_up = lax.ppermute(above[:half] + passed_up, axis, up)
    joined_down = lax.ppermute(below[half:] + passed_down, axis, down)
    return jnp.concatenate([own[:half] + near_down + joined_up, own[half:] + near_up + joined_down], axis=0)


def exchanged(array, axes):
    return lax.all_to_all(array, axes, 0, 0, tiled=True)


def rows_of(array, index):
    return array.at[index].get(mode="promise_in_bounds")


def body(pseudo_grad, outer_params, momentum, save_pages, writer):
    z, y = lax.axis_index("z"), lax.axis_index("y")
    islands = NZ * NY
    entries = pseudo_grad.shape[1] * pseudo_grad.shape[2] * lax.axis_size(TENSOR)

    starts = jnp.cumsum(save_pages) - save_pages
    targets = jnp.arange(islands, dtype=jnp.int32)
    owner_table = writer[None, :] == targets[:, None]
    range_start = jnp.sum(jnp.where(owner_table, starts[None, :], 0), axis=1)
    range_length = jnp.sum(jnp.where(owner_table, save_pages[None, :], 0), axis=1)
    slots = jnp.arange(4, dtype=jnp.int32)
    first_row = (range_start // PER_ROW)[:, None]
    near_row = first_row + (slots[None, :] - first_row) % 4
    held_index = jnp.zeros((islands, 4), jnp.int32)
    sum_index = jnp.zeros((islands, 4), jnp.int32)
    for row in (near_row, near_row + 4):
        tile_row = row // 8
        group = (z - GROUPS * tile_row) % NZ
        page = PER_ROW * row + NY * group + y
        inside = (group < GROUPS) & (page >= range_start[:, None]) & (page < (range_start + range_length)[:, None])
        held_index = jnp.where(inside, row, held_index)
        sum_index = jnp.where(inside, 8 * ((GROUPS * tile_row + group) // NZ) + row % 8, sum_index)
    target_z, target_y = targets // NY, targets % NY
    group = (z - GROUPS * target_z) % NZ
    row_tile = jnp.where(group < GROUPS, (GROUPS * target_z + group) // NZ, 0)
    row_index = (8 * row_tile + 2 * target_y)[:, None] + jnp.arange(2, dtype=jnp.int32)[None, :]
    send_index = jnp.concatenate([sum_index, row_index, jnp.zeros((islands, 2), jnp.int32)], axis=1).reshape(-1)
    is_mine = targets == z * NY + y
    own_start = jnp.sum(jnp.where(is_mine, range_start, 0))
    own_length = jnp.sum(jnp.where(is_mine, range_length, 0))
    place = jnp.arange(208, dtype=jnp.int32)
    page = jnp.minimum(own_start + place, 6655)
    row, block = page // PER_ROW, page % PER_ROW
    source = ((GROUPS * (row // 8) + block // NY) % NZ) * NY + block % NY
    slot = row % 4

    settled = outer_params - (outer_rate * decay_rate * decay_rate) * momentum
    settled = settled.reshape(2, GROUPS, NY, LANES).transpose(1, 2, 0, 3)
    settled = jnp.concatenate([settled, jnp.zeros((NZ - GROUPS, NY, 2, LANES), jnp.float32)], axis=0)
    settled = jnp.concatenate([settled, settled], axis=0)
    spread = lax.dynamic_slice_in_dim(settled, (-GROUPS * z) % NZ, NZ, 0)
    held = exchanged(spread.reshape(islands, 2, LANES), ISLAND).reshape(-1, LANES)
    settled_out = rows_of(held, held_index.reshape(-1)).reshape(islands, 4, LANES)
    settled_in = exchanged(settled_out, ISLAND).reshape(-1, LANES)
    settled_pages = rows_of(settled_in, source * 4 + slot)

    tiles = pseudo_grad[0].reshape(ROW_TILES, 8, GROUPS, NY, LANES).transpose(3, 0, 2, 1, 4)
    over_y = summed_around(tiles.reshape(NY, ROW_TILES * GROUPS, 8, LANES), "y", NY)
    classes = over_y.reshape(GROUPS, 4, 4, 8, LANES).transpose(2, 1, 0, 3, 4)
    windows = summed_around(classes.reshape(4, 4 * GROUPS, 8, LANES), "z", NZ).reshape(4, GROUPS, 8, LANES)
    far = [[4 * h + l for h in range(4)] for l in range(4)]
    summed = lax.all_to_all(windows, "z", 0, 0, tiled=True, axis_index_groups=far).sum(axis=0)
    outer_grad = summed / islands
    part = jnp.sum(outer_grad * outer_grad)

    outgoing = rows_of(outer_grad.reshape(-1, LANES), send_index).reshape(islands, 8, LANES)
    outgoing = jnp.where(jnp.arange(8)[None, :, None] < 6, outgoing, part)
    arrived = exchanged(outgoing, ISLAND)
    over_islands = jnp.sum(arrived[:, 6, 0])
    eight = exchanged(jnp.broadcast_to(over_islands, (lax.axis_size(TENSOR), 1, 1)), TENSOR)
    square_sum = jnp.sum(eight)
    scale = 1.0 / jnp.sqrt(square_sum / entries + epsilon)

    mine = arrived[:, 4:6].reshape(NZ, NY, 2, LANES)
    mine = lax.dynamic_slice_in_dim(jnp.concatenate([mine, mine], axis=0), (GROUPS * z) % NZ, GROUPS, 0)
    normed = mine.transpose(2, 0, 1, 3).reshape(2, -1) * scale
    new_momentum = decay_rate * momentum + normed
    new_master = outer_params - outer_rate * (normed + decay_rate * new_momentum)
    gradient_pages = rows_of(arrived.reshape(-1, LANES), source * 8 + slot)
    pages = settled_pages - (outer_rate * (1.0 + decay_rate)) * (gradient_pages * scale)
    packed = jnp.where((place < own_length)[:, None], pages, 0.0).astype(jnp.bfloat16)
    return (new_master, new_momentum, packed[None])


def solution(mesh):
    split = Mesh(mesh.devices.reshape(NZ, NY, 4, 2), ("z", "y", "x", "core"))
    return jax.shard_map(
        body,
        mesh=split,
        in_specs=(P(ISLAND, None, TENSOR), P(ISLAND, TENSOR), P(ISLAND, TENSOR), P(), P()),
        out_specs=(P(ISLAND, TENSOR), P(ISLAND, TENSOR), P(ISLAND, None, TENSOR)),
        check_vma=False,
    )
```

```python
import jax
import jax.numpy as jnp
from jax import lax
from jax.sharding import Mesh
from jax.sharding import PartitionSpec as P

ISLAND = ("z", "y")
TENSOR = ("x", "core")

epsilon = 1e-06
decay_rate = 0.9
outer_rate = 0.7

NZ, NY, ROW_TILES, GROUPS, LANES = 16, 4, 16, 13, 128
PER_ROW = NY * GROUPS


def shift(n, by):
    return [(i, (i + by) % n) for i in range(n)]


def pick(array, index, axis_size):
    return lax.dynamic_index_in_dim(array, index % axis_size, 0, keepdims=False)


def summed_around(classes, axis, n):
    here = lax.axis_index(axis)
    half = classes.shape[1] // 2
    up, down = shift(n, 1), shift(n, -1)
    far = pick(classes, here + 2, 4)
    passed_up = lax.ppermute(far[:half], axis, up)
    passed_down = lax.ppermute(far[half:], axis, down)
    above, below, own = pick(classes, here + 1, 4), pick(classes, here + 3, 4), pick(classes, here, 4)
    near_up = lax.ppermute(above[half:], axis, up)
    near_down = lax.ppermute(below[:half], axis, down)
    joined_up = lax.ppermute(above[:half] + passed_up, axis, up)
    joined_down = lax.ppermute(below[half:] + passed_down, axis, down)
    return jnp.concatenate([own[:half] + near_down + joined_up, own[half:] + near_up + joined_down], axis=0)


def exchanged(array, axes):
    return lax.all_to_all(array, axes, 0, 0, tiled=True)


def rows_of(array, index):
    return array.at[index].get(mode="promise_in_bounds")


def body(pseudo_grad, outer_params, momentum, save_pages, writer):
    z, y = lax.axis_index("z"), lax.axis_index("y")
    islands = NZ * NY
    entries = pseudo_grad.shape[1] * pseudo_grad.shape[2] * lax.axis_size(TENSOR)

    starts = jnp.cumsum(save_pages) - save_pages
    targets = jnp.arange(islands, dtype=jnp.int32)
    owner_table = writer[None, :] == targets[:, None]
    range_start = jnp.sum(jnp.where(owner_table, starts[None, :], 0), axis=1)
    range_length = jnp.sum(jnp.where(owner_table, save_pages[None, :], 0), axis=1)
    slots = jnp.arange(4, dtype=jnp.int32)
    first_row = (range_start // PER_ROW)[:, None]
    near_row = first_row + (slots[None, :] - first_row) % 4
    held_index = jnp.zeros((islands, 4), jnp.int32)
    sum_index = jnp.zeros((islands, 4), jnp.int32)
    for row in (near_row, near_row + 4):
        tile_row = row // 8
        group = (z - GROUPS * tile_row) % NZ
        page = PER_ROW * row + NY * group + y
        inside = (group < GROUPS) & (page >= range_start[:, None]) & (page < (range_start + range_length)[:, None])
        held_index = jnp.where(inside, row, held_index)
        sum_index = jnp.where(inside, 8 * ((GROUPS * tile_row + group) // NZ) + row % 8, sum_index)
    target_z, target_y = targets // NY, targets % NY
    group = (z - GROUPS * target_z) % NZ
    row_tile = jnp.where(group < GROUPS, (GROUPS * target_z + group) // NZ, 0)
    row_index = (8 * row_tile + 2 * target_y)[:, None] + jnp.arange(2, dtype=jnp.int32)[None, :]
    send_index = jnp.concatenate([sum_index, row_index, jnp.zeros((islands, 2), jnp.int32)], axis=1).reshape(-1)
    is_mine = targets == z * NY + y
    own_start = jnp.sum(jnp.where(is_mine, range_start, 0))
    own_length = jnp.sum(jnp.where(is_mine, range_length, 0))
    place = jnp.arange(208, dtype=jnp.int32)
    page = jnp.minimum(own_start + place, 6655)
    row, block = page // PER_ROW, page % PER_ROW
    source = ((GROUPS * (row // 8) + block // NY) % NZ) * NY + block % NY
    slot = row % 4

    settled = outer_params - (outer_rate * decay_rate * decay_rate) * momentum
    settled = settled.reshape(2, GROUPS, NY, LANES).transpose(1, 2, 0, 3)
    settled = jnp.concatenate([settled, jnp.zeros((NZ - GROUPS, NY, 2, LANES), jnp.float32)], axis=0)
    settled = jnp.concatenate([settled, settled], axis=0)
    spread = lax.dynamic_slice_in_dim(settled, (-GROUPS * z) % NZ, NZ, 0)
    held = exchanged(spread.reshape(islands, 2, LANES), ISLAND).reshape(-1, LANES)
    settled_out = rows_of(held, held_index.reshape(-1)).reshape(islands, 4, LANES)
    settled_in = exchanged(settled_out, ISLAND).reshape(-1, LANES)

    tiles = pseudo_grad[0].reshape(ROW_TILES, 8, GROUPS, NY, LANES).transpose(3, 0, 2, 1, 4)
    over_y = summed_around(tiles.reshape(NY, ROW_TILES * GROUPS, 8, LANES), "y", NY)
    over_y, settled_in = lax.optimization_barrier((over_y, settled_in))
    settled_pages = rows_of(settled_in, source * 4 + slot)
    classes = over_y.reshape(GROUPS, 4, 4, 8, LANES).transpose(2, 1, 0, 3, 4)
    windows = summed_around(classes.reshape(4, 4 * GROUPS, 8, LANES), "z", NZ).reshape(4, GROUPS, 8, LANES)
    far = [[4 * h + l for h in range(4)] for l in range(4)]
    summed = lax.all_to_all(windows, "z", 0, 0, tiled=True, axis_index_groups=far).sum(axis=0)
    outer_grad = summed / islands
    part = jnp.sum(outer_grad * outer_grad)

    outgoing = rows_of(outer_grad.reshape(-1, LANES), send_index).reshape(islands, 8, LANES)
    outgoing = jnp.where(jnp.arange(8)[None, :, None] < 6, outgoing, part)
    arrived = exchanged(outgoing, ISLAND)
    over_islands = jnp.sum(arrived[:, 6, 0])
    eight = exchanged(jnp.broadcast_to(over_islands, (lax.axis_size(TENSOR), 1, 1)), TENSOR)
    square_sum = jnp.sum(eight)
    scale = 1.0 / jnp.sqrt(square_sum / entries + epsilon)

    mine = arrived[:, 4:6].reshape(NZ, NY, 2, LANES)
    mine = lax.dynamic_slice_in_dim(jnp.concatenate([mine, mine], axis=0), (GROUPS * z) % NZ, GROUPS, 0)
    normed = mine.transpose(2, 0, 1, 3).reshape(2, -1) * scale
    new_momentum = decay_rate * momentum + normed
    new_master = outer_params - outer_rate * (normed + decay_rate * new_momentum)
    gradient_pages = rows_of(arrived.reshape(-1, LANES), source * 8 + slot)
    pages = settled_pages - (outer_rate * (1.0 + decay_rate)) * (gradient_pages * scale)
    packed = jnp.where((place < own_length)[:, None], pages, 0.0).astype(jnp.bfloat16)
    return (new_master, new_momentum, packed[None])


def solution(mesh):
    split = Mesh(mesh.devices.reshape(NZ, NY, 4, 2), ("z", "y", "x", "core"))
    return jax.shard_map(
        body,
        mesh=split,
        in_specs=(P(ISLAND, None, TENSOR), P(ISLAND, TENSOR), P(ISLAND, TENSOR), P(), P()),
        out_specs=(P(ISLAND, TENSOR), P(ISLAND, TENSOR), P(ISLAND, None, TENSOR)),
        check_vma=False,
    )
```

```python
import jax
import jax.numpy as jnp
from jax import lax
from jax.experimental import pallas as pl
from jax.experimental.pallas import tpu as pltpu
from jax.sharding import Mesh
from jax.sharding import PartitionSpec as P

ISLAND = ("z", "y")
TENSOR = ("x", "core")

epsilon = 1e-06
decay_rate = 0.9
outer_rate = 0.7

NZ, NY, ROW_TILES, GROUPS, LANES = 16, 4, 16, 13, 128
PER_ROW = NY * GROUPS
IN_VMEM = pl.BlockSpec(memory_space=pltpu.VMEM)
ROWS_SENT, HELD_FROM, PART_AT = 12, 104, 232


def shift(n, by):
    return [(i, (i + by) % n) for i in range(n)]


def pick(array, index, axis_size):
    return lax.dynamic_index_in_dim(array, index % axis_size, 0, keepdims=False)


def summed_around(class_of, riders, axis, n):
    here = lax.axis_index(axis)
    far = class_of(here + 2)
    half = far.shape[0] // 2
    up, down = shift(n, 1), shift(n, -1)
    join = lambda *parts: jnp.concatenate(parts, axis=0)
    passed_up = lax.ppermute(join(far[:half], pick(riders, here + 2, n)), axis, up)
    passed_down = lax.ppermute(far[half:], axis, down)
    above, below, own = class_of(here + 1), class_of(here + 3), class_of(here)
    near_up = lax.ppermute(join(above[half:], pick(riders, here + 1, n)), axis, up)
    near_down = lax.ppermute(join(below[:half], pick(riders, here + 3, n)), axis, down)
    for_above, for_below = lax.optimization_barrier(
        (join(above[:half] + passed_up[:half], passed_up[half:]), below[half:] + passed_down)
    )
    joined_up = lax.ppermute(for_above, axis, up)
    joined_down = lax.ppermute(for_below, axis, down)
    own, near_up, near_down, joined_up, joined_down = lax.optimization_barrier(
        (own, near_up, near_down, joined_up, joined_down)
    )
    total = join(own[:half] + near_down[:half] + joined_up[:half], own[half:] + near_up[:half] + joined_down)
    senders = jnp.stack([pick(riders, here, n), near_down[half:], joined_up[half:], near_up[half:]])
    return total, rolled(senders, n - here)


def summed_in_window(classes, riders, axis, n):
    here = lax.axis_index(axis)
    half, whole = classes.shape[1] // 2, classes.shape[1]
    join = lambda *parts: jnp.concatenate(parts, axis=0)
    far = pick(classes, here + 2, 4)
    far_up = lax.ppermute(join(far[:half], pick(riders, here + 2, 4)), axis, shift(n, 2))
    far_down = lax.ppermute(far[half:], axis, shift(n, -2))
    near_up = lax.ppermute(join(pick(classes, here + 1, 4), pick(riders, here + 1, 4)), axis, shift(n, 1))
    near_down = lax.ppermute(join(pick(classes, here + 3, 4), pick(riders, here + 3, 4)), axis, shift(n, -1))
    return pl.pallas_call(
        window_kernel,
        out_shape=jax.ShapeDtypeStruct((4, GROUPS + 4, 8, LANES), jnp.float32),
        in_specs=[IN_VMEM] * 6,
        out_specs=IN_VMEM,
        compiler_params=pltpu.CompilerParams(vmem_limit_bytes=4 << 20),
    )(pick(classes, here, 4), pick(riders, here, 4), near_up, near_down, far_up, far_down)


def window_kernel(own, rider, near_up, near_down, far_up, far_down, out):
    for chunk in range(4):
        at = pl.ds(GROUPS * chunk, GROUPS)
        far = far_up if chunk < 2 else far_down
        out[chunk, :GROUPS] = own[at] + near_up[at] + near_down[at] + far[pl.ds(GROUPS * (chunk % 2), GROUPS)]
        out[chunk, GROUPS] = rider[chunk]
        out[chunk, GROUPS + 1] = near_up[4 * GROUPS + chunk]
        out[chunk, GROUPS + 2] = near_down[4 * GROUPS + chunk]
        out[chunk, GROUPS + 3] = far_up[2 * GROUPS + chunk]


def table_kernel(windows, out):
    mean = (windows[0, :GROUPS] + windows[1, :GROUPS] + windows[2, :GROUPS] + windows[3, :GROUPS]) / (NZ * NY)
    out[:GROUPS] = mean
    for chunk in range(4):
        out[pl.ds(GROUPS + 4 * chunk, 4)] = windows[chunk, GROUPS:]
    out[GROUPS + 16] = jnp.full((8, LANES), jnp.sum(mean * mean), jnp.float32)


def rolled(array, by):
    n = array.shape[0]
    return lax.dynamic_slice_in_dim(jnp.concatenate([array, array], axis=0), by % n, n, 0)


def exchanged(array, axes):
    return lax.all_to_all(array, axes, 0, 0, tiled=True)


def rows_of(array, index):
    return array.at[index].get(mode="promise_in_bounds")


def body(pseudo_grad, outer_params, momentum, save_pages, writer):
    z, y = lax.axis_index("z"), lax.axis_index("y")
    islands = NZ * NY
    entries = pseudo_grad.shape[1] * pseudo_grad.shape[2] * lax.axis_size(TENSOR)

    order = jnp.arange(islands, dtype=jnp.int32)[:, None]

    def window_of(target):
        hit = writer[:, None] == target[None, :]
        position = jnp.sum(jnp.where(hit, order, 0), axis=0)
        length = jnp.sum(jnp.where(hit, save_pages[:, None], 0), axis=0)
        return jnp.sum(jnp.where(order < position[None, :], save_pages[:, None], 0), axis=0), length

    def page_for(target, slot):
        start, length = window_of(target)
        first_row = start // PER_ROW
        near_row = first_row + (slot - first_row) % 4
        held, local = jnp.zeros_like(target), jnp.zeros_like(target)
        for row in (near_row, near_row + 4):
            tile = GROUPS * (row // 8)
            group = (z - tile) % NZ
            page = PER_ROW * row + NY * group + y
            inside = (group < GROUPS) & (page >= start) & (page < start + length)
            apart = (row // 8 - z % 4) % NZ
            sender = jnp.where(apart % 4 == 0, 0, jnp.where(apart % 4 == 1, 2, jnp.where(apart % 4 == 2, 3, 1)))
            held = jnp.where(inside, 32 * ((apart + 2) // 4 % 4) + 8 * sender + row % 8, held)
            local = jnp.where(inside, 8 * ((tile + group) // NZ) + row % 8, local)
        return held, local

    flat = jnp.arange(ROWS_SENT * islands, dtype=jnp.int32)
    target, kind = flat // ROWS_SENT, flat % ROWS_SENT
    held_index, sum_index = page_for(target, kind % 4)
    tile = GROUPS * (target // NY)
    group = (z - tile) % NZ
    row_index = jnp.where(group < GROUPS, 8 * ((tile + group) // NZ), 0) + 2 * (target % NY) + kind % 2
    send_index = jnp.where(kind < 4, sum_index, jnp.where(kind < 8, HELD_FROM + held_index, row_index))
    send_index = jnp.where(kind < 10, send_index, PART_AT)
    own_start, own_length = window_of((z * NY + y)[None])
    place = jnp.arange(208, dtype=jnp.int32)
    page = jnp.minimum(own_start + place, 6655)
    row, block = page // PER_ROW, page % PER_ROW
    source = ((GROUPS * (row // 8) + block // NY) % NZ) * NY + block % NY
    slot = row % 4

    settled = outer_params - (outer_rate * decay_rate * decay_rate) * momentum
    settled = settled.reshape(2, GROUPS, NY, LANES).transpose(2, 1, 0, 3)
    settled = jnp.concatenate([settled, jnp.zeros((NY, NZ - GROUPS, 2, LANES), jnp.float32)], axis=1)

    by_block = pseudo_grad[0].reshape(ROW_TILES, 8, GROUPS, NY, LANES)

    def block_class(index):
        taken = lax.dynamic_index_in_dim(by_block, index % NY, 3, keepdims=False)
        return taken.transpose(0, 2, 1, 3).reshape(ROW_TILES * GROUPS, 8, LANES)

    over_y, settled = summed_around(block_class, settled.reshape(NY, 4, 8, LANES), "y", NY)
    settled = settled.reshape(NY, NZ, 2, LANES).transpose(1, 0, 2, 3).reshape(NZ, 8, LANES)
    settled = rolled(settled, -GROUPS * z).reshape(4, 4, 8, LANES).transpose(1, 0, 2, 3)
    classes = over_y.reshape(GROUPS, 4, 4, 8, LANES).transpose(2, 1, 0, 3, 4)
    windows = summed_in_window(classes.reshape(4, 4 * GROUPS, 8, LANES), settled, "z", NZ)
    far = [[4 * h + l for h in range(4)] for l in range(4)]
    windows = lax.all_to_all(windows, "z", 0, 0, tiled=True, axis_index_groups=far)
    table = pl.pallas_call(
        table_kernel,
        out_shape=jax.ShapeDtypeStruct((GROUPS + 17, 8, LANES), jnp.float32),
        in_specs=[IN_VMEM],
        out_specs=IN_VMEM,
        compiler_params=pltpu.CompilerParams(vmem_limit_bytes=4 << 20),
    )(windows).reshape(-1, LANES)

    outgoing = rows_of(table, send_index).reshape(-1, 4, LANES)
    arrived = exchanged(outgoing, ISLAND).reshape(islands, 3, 4, LANES)
    over_islands = jnp.sum(arrived[:, 2, 2], axis=0)
    eight = exchanged(jnp.broadcast_to(over_islands, (lax.axis_size(TENSOR), 1, LANES)), TENSOR)
    square_sum = jnp.sum(eight, axis=0)
    scale = 1.0 / jnp.sqrt(square_sum / entries + epsilon)

    mine = arrived[:, 2, :2].reshape(NZ, NY, 2, LANES)
    mine = lax.dynamic_slice_in_dim(jnp.concatenate([mine, mine], axis=0), (GROUPS * z) % NZ, GROUPS, 0)
    normed = (mine.transpose(2, 0, 1, 3) * scale).reshape(2, -1)
    new_momentum = decay_rate * momentum + normed
    new_master = outer_params - outer_rate * (normed + decay_rate * new_momentum)
    arrived = arrived.reshape(-1, LANES)
    gradient_pages = rows_of(arrived, source * ROWS_SENT + slot)
    settled_pages = rows_of(arrived, source * ROWS_SENT + 4 + slot)
    pages = settled_pages - (outer_rate * (1.0 + decay_rate)) * (gradient_pages * scale)
    packed = jnp.where((place < own_length)[:, None], pages, 0.0).astype(jnp.bfloat16)
    return (new_master, new_momentum, packed[None])


def solution(mesh):
    split = Mesh(mesh.devices.reshape(NZ, NY, 4, 2), ("z", "y", "x", "core"))
    return jax.shard_map(
        body,
        mesh=split,
        in_specs=(P(ISLAND, None, TENSOR), P(ISLAND, TENSOR), P(ISLAND, TENSOR), P(), P()),
        out_specs=(P(ISLAND, TENSOR), P(ISLAND, TENSOR), P(ISLAND, None, TENSOR)),
        check_vma=False,
    )
```

```python
import jax
import jax.numpy as jnp
from jax import lax
from jax.experimental import pallas as pl
from jax.experimental.pallas import tpu as pltpu
from jax.sharding import Mesh
from jax.sharding import PartitionSpec as P

ISLAND = ("z", "y")
TENSOR = ("x", "core")

epsilon = 1e-06
decay_rate = 0.9
outer_rate = 0.7

NZ, NY, ROW_TILES, GROUPS, LANES = 16, 4, 16, 13, 128
PER_ROW = NY * GROUPS
TENSOR_SIZE = 8
ENTRIES = 8 * ROW_TILES * PER_ROW * LANES * TENSOR_SIZE
IN_VMEM = pl.BlockSpec(memory_space=pltpu.VMEM)
ROWS_SENT, HELD_FROM, PART_AT = 11, 104, 232


def shift(n, by):
    return [(i, (i + by) % n) for i in range(n)]


def pick(array, index, axis_size):
    return lax.dynamic_index_in_dim(array, index % axis_size, 0, keepdims=False)


def summed_around(class_of, riders, axis, n):
    here = lax.axis_index(axis)
    far = class_of(here + 2)
    half = far.shape[0] // 2
    up, down = shift(n, 1), shift(n, -1)
    join = lambda *parts: jnp.concatenate(parts, axis=0)
    passed_up = lax.ppermute(join(far[:half], pick(riders, here + 2, n)), axis, up)
    passed_down = lax.ppermute(far[half:], axis, down)
    above, below, own = class_of(here + 1), class_of(here + 3), class_of(here)
    near_up = lax.ppermute(join(above[half:], pick(riders, here + 1, n)), axis, up)
    near_down = lax.ppermute(join(below[:half], pick(riders, here + 3, n)), axis, down)
    for_above, for_below = lax.optimization_barrier(
        (join(above[:half] + passed_up[:half], passed_up[half:]), below[half:] + passed_down)
    )
    joined_up = lax.ppermute(for_above, axis, up)
    joined_down = lax.ppermute(for_below, axis, down)
    own, near_up, near_down, joined_up, joined_down = lax.optimization_barrier(
        (own, near_up, near_down, joined_up, joined_down)
    )
    total = join(own[:half] + near_down[:half] + joined_up[:half], own[half:] + near_up[:half] + joined_down)
    senders = jnp.stack([pick(riders, here, n), near_down[half:], joined_up[half:], near_up[half:]])
    return total, rolled(senders, n - here)


def summed_in_window(classes, riders, axis, n):
    here = lax.axis_index(axis)
    half, whole = classes.shape[1] // 2, classes.shape[1]
    join = lambda *parts: jnp.concatenate(parts, axis=0)
    far = pick(classes, here + 2, 4)
    far_up = lax.ppermute(join(far[:half], pick(riders, here + 2, 4)), axis, shift(n, 2))
    far_down = lax.ppermute(far[half:], axis, shift(n, -2))
    near_up = lax.ppermute(join(pick(classes, here + 1, 4), pick(riders, here + 1, 4)), axis, shift(n, 1))
    near_down = lax.ppermute(join(pick(classes, here + 3, 4), pick(riders, here + 3, 4)), axis, shift(n, -1))
    return pl.pallas_call(
        window_kernel,
        out_shape=jax.ShapeDtypeStruct((4, GROUPS + 4, 8, LANES), jnp.float32),
        in_specs=[IN_VMEM] * 6,
        out_specs=IN_VMEM,
        compiler_params=pltpu.CompilerParams(vmem_limit_bytes=4 << 20),
    )(pick(classes, here, 4), pick(riders, here, 4), near_up, near_down, far_up, far_down)


def window_kernel(own, rider, near_up, near_down, far_up, far_down, out):
    for chunk in range(4):
        at = pl.ds(GROUPS * chunk, GROUPS)
        far = far_up if chunk < 2 else far_down
        out[chunk, :GROUPS] = own[at] + near_up[at] + near_down[at] + far[pl.ds(GROUPS * (chunk % 2), GROUPS)]
        out[chunk, GROUPS] = rider[chunk]
        out[chunk, GROUPS + 1] = near_up[4 * GROUPS + chunk]
        out[chunk, GROUPS + 2] = near_down[4 * GROUPS + chunk]
        out[chunk, GROUPS + 3] = far_up[2 * GROUPS + chunk]


def table_kernel(windows, out):
    mean = (windows[0, :GROUPS] + windows[1, :GROUPS] + windows[2, :GROUPS] + windows[3, :GROUPS]) / (NZ * NY)
    out[:GROUPS] = mean
    for chunk in range(4):
        out[pl.ds(GROUPS + 4 * chunk, 4)] = windows[chunk, GROUPS:]
    out[GROUPS + 16] = jnp.full((8, LANES), jnp.sum(mean * mean), jnp.float32)


def rolled(array, by):
    n = array.shape[0]
    return lax.dynamic_slice_in_dim(jnp.concatenate([array, array], axis=0), by % n, n, 0)


def exchanged(array, axes):
    return lax.all_to_all(array, axes, 0, 0, tiled=True)


def rows_of(array, index):
    return array.at[index].get(mode="promise_in_bounds")


def body(pseudo_grad, outer_params, momentum, save_pages, writer):
    z, y = lax.axis_index("z"), lax.axis_index("y")
    islands = NZ * NY

    order = jnp.arange(islands, dtype=jnp.int32)[:, None]

    def window_of(target):
        hit = writer[:, None] == target[None, :]
        position = jnp.sum(jnp.where(hit, order, 0), axis=0)
        length = jnp.sum(jnp.where(hit, save_pages[:, None], 0), axis=0)
        return jnp.sum(jnp.where(order < position[None, :], save_pages[:, None], 0), axis=0), length

    def page_for(target, slot):
        start, length = window_of(target)
        first_row = start // PER_ROW
        near_row = first_row + (slot - first_row) % 4
        held, local = jnp.zeros_like(target), jnp.zeros_like(target)
        for row in (near_row, near_row + 4):
            tile = GROUPS * (row // 8)
            group = (z - tile) % NZ
            page = PER_ROW * row + NY * group + y
            inside = (group < GROUPS) & (page >= start) & (page < start + length)
            apart = (row // 8 - z % 4) % NZ
            sender = jnp.where(apart % 4 == 0, 0, jnp.where(apart % 4 == 1, 2, jnp.where(apart % 4 == 2, 3, 1)))
            held = jnp.where(inside, 32 * ((apart + 2) // 4 % 4) + 8 * sender + row % 8, held)
            local = jnp.where(inside, 8 * ((tile + group) // NZ) + row % 8, local)
        return held, local

    flat = jnp.arange(ROWS_SENT * islands, dtype=jnp.int32)
    target, kind = flat // ROWS_SENT, flat % ROWS_SENT
    held_index, sum_index = page_for(target, kind % 4)
    tile = GROUPS * (target // NY)
    group = (z - tile) % NZ
    row_index = jnp.where(group < GROUPS, 8 * ((tile + group) // NZ), 0) + 2 * (target % NY) + kind % 2
    send_index = jnp.where(kind < 4, sum_index, jnp.where(kind < 8, HELD_FROM + held_index, row_index))
    send_index = jnp.where(kind < 10, send_index, PART_AT)
    own_start, own_length = window_of((z * NY + y)[None])
    place = jnp.arange(208, dtype=jnp.int32)
    page = jnp.minimum(own_start + place, 6655)
    row, block = page // PER_ROW, page % PER_ROW
    source = ((GROUPS * (row // 8) + block // NY) % NZ) * NY + block % NY
    slot = row % 4

    settled = outer_params - (outer_rate * decay_rate * decay_rate) * momentum
    settled = settled.reshape(2, GROUPS, NY, LANES).transpose(2, 1, 0, 3)
    settled = jnp.concatenate([settled, jnp.zeros((NY, NZ - GROUPS, 2, LANES), jnp.float32)], axis=1)

    by_block = pseudo_grad[0].reshape(ROW_TILES, 8, GROUPS, NY, LANES)

    def block_class(index):
        taken = lax.dynamic_index_in_dim(by_block, index % NY, 3, keepdims=False)
        return taken.transpose(0, 2, 1, 3).reshape(ROW_TILES * GROUPS, 8, LANES)

    over_y, settled = summed_around(block_class, settled.reshape(NY, 4, 8, LANES), "y", NY)
    settled = settled.reshape(NY, NZ, 2, LANES).transpose(1, 0, 2, 3).reshape(NZ, 8, LANES)
    settled = rolled(settled, -GROUPS * z).reshape(4, 4, 8, LANES).transpose(1, 0, 2, 3)
    classes = over_y.reshape(GROUPS, 4, 4, 8, LANES).transpose(2, 1, 0, 3, 4)
    windows = summed_in_window(classes.reshape(4, 4 * GROUPS, 8, LANES), settled, "z", NZ)
    far = [[4 * h + l for h in range(4)] for l in range(4)]
    windows = lax.all_to_all(windows, "z", 0, 0, tiled=True, axis_index_groups=far)
    table = pl.pallas_call(
        table_kernel,
        out_shape=jax.ShapeDtypeStruct((GROUPS + 17, 8, LANES), jnp.float32),
        in_specs=[IN_VMEM],
        out_specs=IN_VMEM,
        compiler_params=pltpu.CompilerParams(vmem_limit_bytes=4 << 20),
    )(windows).reshape(-1, LANES)

    outgoing = rows_of(table, send_index).reshape(-1, 1, LANES)
    arrived = exchanged(outgoing, ISLAND).reshape(-1, LANES)
    over_islands = pl.pallas_call(
        part_kernel,
        out_shape=jax.ShapeDtypeStruct((8, LANES), jnp.float32),
        in_specs=[IN_VMEM],
        out_specs=IN_VMEM,
        compiler_params=pltpu.CompilerParams(vmem_limit_bytes=4 << 20),
    )(arrived)
    eight = exchanged(over_islands.reshape(lax.axis_size(TENSOR), -1, LANES), TENSOR).reshape(-1, LANES)

    flat = jnp.arange(2 * PER_ROW, dtype=jnp.int32)
    even, block = flat // PER_ROW, flat % PER_ROW
    mine = rows_of(arrived, (((GROUPS * z + block // NY) % NZ) * NY + block % NY) * ROWS_SENT + 8 + even).reshape(2, -1)
    gradient_pages = rows_of(arrived, source * ROWS_SENT + slot)
    settled_pages = rows_of(arrived, source * ROWS_SENT + 4 + slot)
    new_master, new_momentum, packed = pl.pallas_call(
        final_kernel,
        out_shape=(
            jax.ShapeDtypeStruct(mine.shape, jnp.float32),
            jax.ShapeDtypeStruct(mine.shape, jnp.float32),
            jax.ShapeDtypeStruct(gradient_pages.shape, jnp.bfloat16),
        ),
        in_specs=[pl.BlockSpec(memory_space=pltpu.SMEM)] + [IN_VMEM] * 6,
        out_specs=(IN_VMEM, IN_VMEM, IN_VMEM),
        compiler_params=pltpu.CompilerParams(vmem_limit_bytes=4 << 20),
    )(own_length, eight, mine, outer_params, momentum, gradient_pages, settled_pages)
    return (new_master, new_momentum, packed[None])


def part_kernel(arrived, out):
    parts = arrived[pl.ds(10, NZ * NY, stride=ROWS_SENT), :]
    out[...] = jnp.broadcast_to(jnp.sum(parts, axis=0, keepdims=True), out.shape)


def final_kernel(length, eight, mine, params, momentum, gradient_pages, settled_pages, master_out, momentum_out, pages_out):
    square_sum = jnp.sum(eight[...], axis=0, keepdims=True) / (eight.shape[0] // TENSOR_SIZE)
    scale = 1.0 / jnp.sqrt(square_sum / ENTRIES + epsilon)
    normed = mine[...] * scale[:, :1]
    new_momentum = decay_rate * momentum[...] + normed
    momentum_out[...] = new_momentum
    master_out[...] = params[...] - outer_rate * (normed + decay_rate * new_momentum)
    pages = settled_pages[...] - (outer_rate * (1.0 + decay_rate)) * (gradient_pages[...] * scale)
    place = lax.broadcasted_iota(jnp.int32, pages.shape, 0)
    pages_out[...] = jnp.where(place < length[0], pages, 0.0).astype(jnp.bfloat16)


def solution(mesh):
    split = Mesh(mesh.devices.reshape(NZ, NY, 4, 2), ("z", "y", "x", "core"))
    return jax.shard_map(
        body,
        mesh=split,
        in_specs=(P(ISLAND, None, TENSOR), P(ISLAND, TENSOR), P(ISLAND, TENSOR), P(), P()),
        out_specs=(P(ISLAND, TENSOR), P(ISLAND, TENSOR), P(ISLAND, None, TENSOR)),
        check_vma=False,
    )
```

```python
import jax
import jax.numpy as jnp
from jax import lax
from jax.experimental import pallas as pl
from jax.experimental.pallas import tpu as pltpu
from jax.sharding import Mesh
from jax.sharding import PartitionSpec as P

ISLAND = ("z", "y")
TENSOR = ("x", "core")

epsilon = 1e-06
decay_rate = 0.9
outer_rate = 0.7

NZ, NY, ROW_TILES, GROUPS, LANES = 16, 4, 16, 13, 128
PER_ROW = NY * GROUPS
TENSOR_SIZE = 8
ENTRIES = 8 * ROW_TILES * PER_ROW * LANES * TENSOR_SIZE
IN_VMEM = pl.BlockSpec(memory_space=pltpu.VMEM)
ROWS_SENT, HELD_FROM, PART_AT = 11, 104, 232


def shift(n, by):
    return [(i, (i + by) % n) for i in range(n)]


def pick(array, index, axis_size):
    return lax.dynamic_index_in_dim(array, index % axis_size, 0, keepdims=False)


def summed_around(class_of, riders, axis, n):
    here = lax.axis_index(axis)
    far = class_of(here + 2)
    half = far.shape[0] // 2
    up, down = shift(n, 1), shift(n, -1)
    join = lambda *parts: jnp.concatenate(parts, axis=0)
    passed_up = lax.ppermute(join(far[:half], pick(riders, here + 2, n)), axis, up)
    passed_down = lax.ppermute(far[half:], axis, down)
    above, below, own = class_of(here + 1), class_of(here + 3), class_of(here)
    near_up = lax.ppermute(join(above[half:], pick(riders, here + 1, n)), axis, up)
    near_down = lax.ppermute(join(below[:half], pick(riders, here + 3, n)), axis, down)
    for_above, for_below = lax.optimization_barrier(
        (join(above[:half] + passed_up[:half], passed_up[half:]), below[half:] + passed_down)
    )
    joined_up = lax.ppermute(for_above, axis, up)
    joined_down = lax.ppermute(for_below, axis, down)
    own, near_up, near_down, joined_up, joined_down = lax.optimization_barrier(
        (own, near_up, near_down, joined_up, joined_down)
    )
    total = join(own[:half] + near_down[:half] + joined_up[:half], own[half:] + near_up[:half] + joined_down)
    senders = jnp.stack([pick(riders, here, n), near_down[half:], joined_up[half:], near_up[half:]])
    return total, rolled(senders, n - here)


def summed_in_window(classes, riders, axis, n):
    here = lax.axis_index(axis)
    half, whole = classes.shape[1] // 2, classes.shape[1]
    join = lambda *parts: jnp.concatenate(parts, axis=0)
    far = pick(classes, here + 2, 4)
    far_up = lax.ppermute(join(far[:half], pick(riders, here + 2, 4)), axis, shift(n, 2))
    far_down = lax.ppermute(far[half:], axis, shift(n, -2))
    near_up = lax.ppermute(join(pick(classes, here + 1, 4), pick(riders, here + 1, 4)), axis, shift(n, 1))
    near_down = lax.ppermute(join(pick(classes, here + 3, 4), pick(riders, here + 3, 4)), axis, shift(n, -1))
    return pl.pallas_call(
        window_kernel,
        out_shape=jax.ShapeDtypeStruct((4, GROUPS + 4, 8, LANES), jnp.float32),
        in_specs=[IN_VMEM] * 6,
        out_specs=IN_VMEM,
        compiler_params=pltpu.CompilerParams(vmem_limit_bytes=4 << 20),
    )(pick(classes, here, 4), pick(riders, here, 4), near_up, near_down, far_up, far_down)


def window_kernel(own, rider, near_up, near_down, far_up, far_down, out):
    for chunk in range(4):
        at = pl.ds(GROUPS * chunk, GROUPS)
        far = far_up if chunk < 2 else far_down
        out[chunk, :GROUPS] = own[at] + near_up[at] + near_down[at] + far[pl.ds(GROUPS * (chunk % 2), GROUPS)]
        out[chunk, GROUPS] = rider[chunk]
        out[chunk, GROUPS + 1] = near_up[4 * GROUPS + chunk]
        out[chunk, GROUPS + 2] = near_down[4 * GROUPS + chunk]
        out[chunk, GROUPS + 3] = far_up[2 * GROUPS + chunk]


def outgoing_kernel(windows, chosen, out):
    mean = (windows[0, :GROUPS] + windows[1, :GROUPS] + windows[2, :GROUPS] + windows[3, :GROUPS]) / (NZ * NY)
    part = jnp.full((1, 8, LANES), jnp.sum(mean * mean), jnp.float32)
    held = [windows[chunk, GROUPS:] for chunk in range(4)]
    rest = jnp.concatenate([mean, *held, part, jnp.zeros((2, 8, LANES), jnp.float32)], axis=0).reshape(256, LANES)
    total = None
    for _ in range(3):
        piece = rest.astype(jnp.bfloat16)
        rest = rest - piece.astype(jnp.float32)
        rows = jnp.dot(chosen[...], piece, preferred_element_type=jnp.float32)
        total = rows if total is None else total + rows
    out[...] = total


def rolled(array, by):
    n = array.shape[0]
    return lax.dynamic_slice_in_dim(jnp.concatenate([array, array], axis=0), by % n, n, 0)


def exchanged(array, axes):
    return lax.all_to_all(array, axes, 0, 0, tiled=True)


def rows_of(array, index):
    return array.at[index].get(mode="promise_in_bounds")


def body(pseudo_grad, outer_params, momentum, save_pages, writer):
    z, y = lax.axis_index("z"), lax.axis_index("y")
    islands = NZ * NY

    order = jnp.arange(islands, dtype=jnp.int32)[:, None]

    def window_of(target):
        hit = writer[:, None] == target[None, :]
        position = jnp.sum(jnp.where(hit, order, 0), axis=0)
        length = jnp.sum(jnp.where(hit, save_pages[:, None], 0), axis=0)
        return jnp.sum(jnp.where(order < position[None, :], save_pages[:, None], 0), axis=0), length

    def page_for(target, slot):
        start, length = window_of(target)
        first_row = start // PER_ROW
        near_row = first_row + (slot - first_row) % 4
        held, local = jnp.zeros_like(target), jnp.zeros_like(target)
        for row in (near_row, near_row + 4):
            tile = GROUPS * (row // 8)
            group = (z - tile) % NZ
            page = PER_ROW * row + NY * group + y
            inside = (group < GROUPS) & (page >= start) & (page < start + length)
            apart = (row // 8 - z % 4) % NZ
            sender = jnp.where(apart % 4 == 0, 0, jnp.where(apart % 4 == 1, 2, jnp.where(apart % 4 == 2, 3, 1)))
            held = jnp.where(inside, 32 * ((apart + 2) // 4 % 4) + 8 * sender + row % 8, held)
            local = jnp.where(inside, 8 * ((tile + group) // NZ) + row % 8, local)
        return held, local

    flat = jnp.arange(ROWS_SENT * islands, dtype=jnp.int32)
    target, kind = flat // ROWS_SENT, flat % ROWS_SENT
    held_index, sum_index = page_for(target, kind % 4)
    tile = GROUPS * (target // NY)
    group = (z - tile) % NZ
    row_index = jnp.where(group < GROUPS, 8 * ((tile + group) // NZ), 0) + 2 * (target % NY) + kind % 2
    send_index = jnp.where(kind < 4, sum_index, jnp.where(kind < 8, HELD_FROM + held_index, row_index))
    send_index = jnp.where(kind < 10, send_index, PART_AT)
    own_start, own_length = window_of((z * NY + y)[None])
    place = jnp.arange(208, dtype=jnp.int32)
    page = jnp.minimum(own_start + place, 6655)
    row, block = page // PER_ROW, page % PER_ROW
    source = ((GROUPS * (row // 8) + block // NY) % NZ) * NY + block % NY
    slot = row % 4

    settled = outer_params - (outer_rate * decay_rate * decay_rate) * momentum
    settled = settled.reshape(2, GROUPS, NY, LANES).transpose(2, 1, 0, 3)
    settled = jnp.concatenate([settled, jnp.zeros((NY, NZ - GROUPS, 2, LANES), jnp.float32)], axis=1)

    by_block = pseudo_grad[0].reshape(ROW_TILES, 8, GROUPS, NY, LANES)

    def block_class(index):
        taken = lax.dynamic_index_in_dim(by_block, index % NY, 3, keepdims=False)
        return taken.transpose(0, 2, 1, 3).reshape(ROW_TILES * GROUPS, 8, LANES)

    over_y, settled = summed_around(block_class, settled.reshape(NY, 4, 8, LANES), "y", NY)
    settled = settled.reshape(NY, NZ, 2, LANES).transpose(1, 0, 2, 3).reshape(NZ, 8, LANES)
    settled = rolled(settled, -GROUPS * z).reshape(4, 4, 8, LANES).transpose(1, 0, 2, 3)
    classes = over_y.reshape(GROUPS, 4, 4, 8, LANES).transpose(2, 1, 0, 3, 4)
    windows = summed_in_window(classes.reshape(4, 4 * GROUPS, 8, LANES), settled, "z", NZ)
    far = [[4 * h + l for h in range(4)] for l in range(4)]
    windows = lax.all_to_all(windows, "z", 0, 0, tiled=True, axis_index_groups=far)
    chosen = (send_index[:, None] == jnp.arange(256, dtype=jnp.int32)[None, :]).astype(jnp.bfloat16)

    outgoing = pl.pallas_call(
        outgoing_kernel,
        out_shape=jax.ShapeDtypeStruct((ROWS_SENT * islands, LANES), jnp.float32),
        in_specs=[IN_VMEM] * 2,
        out_specs=IN_VMEM,
        compiler_params=pltpu.CompilerParams(vmem_limit_bytes=6 << 20),
    )(windows, chosen)
    arrived = exchanged(outgoing.reshape(-1, 1, LANES), ISLAND).reshape(-1, LANES)
    over_islands = pl.pallas_call(
        part_kernel,
        out_shape=jax.ShapeDtypeStruct((8, LANES), jnp.float32),
        in_specs=[IN_VMEM],
        out_specs=IN_VMEM,
        compiler_params=pltpu.CompilerParams(vmem_limit_bytes=4 << 20),
    )(arrived)
    eight = exchanged(over_islands.reshape(lax.axis_size(TENSOR), -1, LANES), TENSOR).reshape(-1, LANES)

    flat = jnp.arange(2 * PER_ROW, dtype=jnp.int32)
    even, block = flat // PER_ROW, flat % PER_ROW
    mine = rows_of(arrived, (((GROUPS * z + block // NY) % NZ) * NY + block % NY) * ROWS_SENT + 8 + even).reshape(2, -1)
    gradient_pages = rows_of(arrived, source * ROWS_SENT + slot)
    settled_pages = rows_of(arrived, source * ROWS_SENT + 4 + slot)
    new_master, new_momentum, packed = pl.pallas_call(
        final_kernel,
        out_shape=(
            jax.ShapeDtypeStruct(mine.shape, jnp.float32),
            jax.ShapeDtypeStruct(mine.shape, jnp.float32),
            jax.ShapeDtypeStruct(gradient_pages.shape, jnp.bfloat16),
        ),
        in_specs=[pl.BlockSpec(memory_space=pltpu.SMEM)] + [IN_VMEM] * 6,
        out_specs=(IN_VMEM, IN_VMEM, IN_VMEM),
        compiler_params=pltpu.CompilerParams(vmem_limit_bytes=4 << 20),
    )(own_length, eight, mine, outer_params, momentum, gradient_pages, settled_pages)
    return (new_master, new_momentum, packed[None])


def part_kernel(arrived, out):
    parts = arrived[pl.ds(10, NZ * NY, stride=ROWS_SENT), :]
    out[...] = jnp.broadcast_to(jnp.sum(parts, axis=0, keepdims=True), out.shape)


def final_kernel(length, eight, mine, params, momentum, gradient_pages, settled_pages, master_out, momentum_out, pages_out):
    square_sum = jnp.sum(eight[...], axis=0, keepdims=True) / (eight.shape[0] // TENSOR_SIZE)
    scale = 1.0 / jnp.sqrt(square_sum / ENTRIES + epsilon)
    normed = mine[...] * scale[:, :1]
    new_momentum = decay_rate * momentum[...] + normed
    momentum_out[...] = new_momentum
    master_out[...] = params[...] - outer_rate * (normed + decay_rate * new_momentum)
    pages = settled_pages[...] - (outer_rate * (1.0 + decay_rate)) * (gradient_pages[...] * scale)
    place = lax.broadcasted_iota(jnp.int32, pages.shape, 0)
    pages_out[...] = jnp.where(place < length[0], pages, 0.0).astype(jnp.bfloat16)


def solution(mesh):
    split = Mesh(mesh.devices.reshape(NZ, NY, 4, 2), ("z", "y", "x", "core"))
    return jax.shard_map(
        body,
        mesh=split,
        in_specs=(P(ISLAND, None, TENSOR), P(ISLAND, TENSOR), P(ISLAND, TENSOR), P(), P()),
        out_specs=(P(ISLAND, TENSOR), P(ISLAND, TENSOR), P(ISLAND, None, TENSOR)),
        check_vma=False,
    )
```

```python
import jax
import jax.numpy as jnp
from jax import lax
from jax.experimental import pallas as pl
from jax.experimental.pallas import tpu as pltpu
from jax.sharding import Mesh
from jax.sharding import PartitionSpec as P

ISLAND = ("z", "y")
TENSOR = ("x", "core")

epsilon = 1e-06
decay_rate = 0.9
outer_rate = 0.7

NZ, NY, ROW_TILES, GROUPS, LANES = 16, 4, 16, 13, 128
PER_ROW = NY * GROUPS
TENSOR_SIZE = 8
ENTRIES = 8 * ROW_TILES * PER_ROW * LANES * TENSOR_SIZE
IN_VMEM = pl.BlockSpec(memory_space=pltpu.VMEM)
ROWS_SENT, HELD_FROM, PART_AT = 11, 104, 232


def shift(n, by):
    return [(i, (i + by) % n) for i in range(n)]


def pick(array, index, axis_size):
    return lax.dynamic_index_in_dim(array, index % axis_size, 0, keepdims=False)


def summed_around(class_of, riders, axis, n):
    here = lax.axis_index(axis)
    far = class_of(here + 2)
    half = far.shape[0] // 2
    up, down = shift(n, 1), shift(n, -1)
    join = lambda *parts: jnp.concatenate(parts, axis=0)
    passed_up = lax.ppermute(join(far[:half], pick(riders, here + 2, n)), axis, up)
    passed_down = lax.ppermute(far[half:], axis, down)
    above, below, own = class_of(here + 1), class_of(here + 3), class_of(here)
    near_up = lax.ppermute(join(above[half:], pick(riders, here + 1, n)), axis, up)
    near_down = lax.ppermute(join(below[:half], pick(riders, here + 3, n)), axis, down)
    for_above, for_below = lax.optimization_barrier(
        (join(above[:half] + passed_up[:half], passed_up[half:]), below[half:] + passed_down)
    )
    joined_up = lax.ppermute(for_above, axis, up)
    joined_down = lax.ppermute(for_below, axis, down)
    own, near_up, near_down, joined_up, joined_down = lax.optimization_barrier(
        (own, near_up, near_down, joined_up, joined_down)
    )
    total = join(own[:half] + near_down[:half] + joined_up[:half], own[half:] + near_up[:half] + joined_down)
    senders = jnp.stack([pick(riders, here, n), near_down[half:], joined_up[half:], near_up[half:]])
    return total, rolled(senders, n - here)


def summed_in_window(classes, riders, axis, n):
    here = lax.axis_index(axis)
    half, whole = classes.shape[1] // 2, classes.shape[1]
    join = lambda *parts: jnp.concatenate(parts, axis=0)
    far = pick(classes, here + 2, 4)
    far_up = lax.ppermute(join(far[:half], pick(riders, here + 2, 4)), axis, shift(n, 2))
    far_down = lax.ppermute(far[half:], axis, shift(n, -2))
    near_up = lax.ppermute(join(pick(classes, here + 1, 4), pick(riders, here + 1, 4)), axis, shift(n, 1))
    near_down = lax.ppermute(join(pick(classes, here + 3, 4), pick(riders, here + 3, 4)), axis, shift(n, -1))
    return pl.pallas_call(
        window_kernel,
        out_shape=jax.ShapeDtypeStruct((4, GROUPS + 4, 8, LANES), jnp.float32),
        in_specs=[IN_VMEM] * 6,
        out_specs=IN_VMEM,
        compiler_params=pltpu.CompilerParams(vmem_limit_bytes=4 << 20),
    )(pick(classes, here, 4), pick(riders, here, 4), near_up, near_down, far_up, far_down)


def window_kernel(own, rider, near_up, near_down, far_up, far_down, out):
    for chunk in range(4):
        at = pl.ds(GROUPS * chunk, GROUPS)
        far = far_up if chunk < 2 else far_down
        out[chunk, :GROUPS] = own[at] + near_up[at] + near_down[at] + far[pl.ds(GROUPS * (chunk % 2), GROUPS)]
        out[chunk, GROUPS] = rider[chunk]
        out[chunk, GROUPS + 1] = near_up[4 * GROUPS + chunk]
        out[chunk, GROUPS + 2] = near_down[4 * GROUPS + chunk]
        out[chunk, GROUPS + 3] = far_up[2 * GROUPS + chunk]


def outgoing_kernel(windows, chosen, out):
    mean = (windows[0, :GROUPS] + windows[1, :GROUPS] + windows[2, :GROUPS] + windows[3, :GROUPS]) / (NZ * NY)
    part = jnp.full((1, 8, LANES), jnp.sum(mean * mean), jnp.float32)
    held = [windows[chunk, GROUPS:] for chunk in range(4)]
    rest = jnp.concatenate([mean, *held, part, jnp.zeros((2, 8, LANES), jnp.float32)], axis=0).reshape(256, LANES)
    total = None
    for _ in range(3):
        piece = rest.astype(jnp.bfloat16)
        rest = rest - piece.astype(jnp.float32)
        rows = jnp.dot(chosen[...], piece, preferred_element_type=jnp.float32)
        total = rows if total is None else total + rows
    out[...] = total


def rolled(array, by):
    n = array.shape[0]
    return lax.dynamic_slice_in_dim(jnp.concatenate([array, array], axis=0), by % n, n, 0)


def exchanged(array, axes):
    return lax.all_to_all(array, axes, 0, 0, tiled=True)


def rows_of(array, index):
    return array.at[index].get(mode="promise_in_bounds")


def body(pseudo_grad, outer_params, momentum, save_pages, writer):
    z, y = lax.axis_index("z"), lax.axis_index("y")
    islands = NZ * NY

    order = jnp.arange(islands, dtype=jnp.int32)[:, None]

    def window_of(target):
        hit = writer[:, None] == target[None, :]
        position = jnp.sum(jnp.where(hit, order, 0), axis=0)
        length = jnp.sum(jnp.where(hit, save_pages[:, None], 0), axis=0)
        return jnp.sum(jnp.where(order < position[None, :], save_pages[:, None], 0), axis=0), length

    def page_for(target, slot):
        start, length = window_of(target)
        first_row = start // PER_ROW
        near_row = first_row + (slot - first_row) % 4
        held, local = jnp.zeros_like(target), jnp.zeros_like(target)
        for row in (near_row, near_row + 4):
            tile = GROUPS * (row // 8)
            group = (z - tile) % NZ
            page = PER_ROW * row + NY * group + y
            inside = (group < GROUPS) & (page >= start) & (page < start + length)
            apart = (row // 8 - z % 4) % NZ
            sender = jnp.where(apart % 4 == 0, 0, jnp.where(apart % 4 == 1, 2, jnp.where(apart % 4 == 2, 3, 1)))
            held = jnp.where(inside, 32 * ((apart + 2) // 4 % 4) + 8 * sender + row % 8, held)
            local = jnp.where(inside, 8 * ((tile + group) // NZ) + row % 8, local)
        return held, local

    flat = jnp.arange(ROWS_SENT * islands, dtype=jnp.int32)
    target, kind = flat // ROWS_SENT, flat % ROWS_SENT
    held_index, sum_index = page_for(target, (kind + 3) % 4)
    tile = GROUPS * (target // NY)
    group = (z - tile) % NZ
    row_index = jnp.where(group < GROUPS, 8 * ((tile + group) // NZ), 0) + 2 * (target % NY) + (kind + 1) % 2
    send_index = jnp.where(kind < 5, sum_index, jnp.where(kind < 9, HELD_FROM + held_index, row_index))
    send_index = jnp.where(kind > 0, send_index, PART_AT)
    own_start, own_length = window_of((z * NY + y)[None])
    place = jnp.arange(208, dtype=jnp.int32)
    page = jnp.minimum(own_start + place, 6655)
    row, block = page // PER_ROW, page % PER_ROW
    source = ((GROUPS * (row // 8) + block // NY) % NZ) * NY + block % NY
    slot = row % 4

    settled = outer_params - (outer_rate * decay_rate * decay_rate) * momentum
    settled = settled.reshape(2, GROUPS, NY, LANES).transpose(2, 1, 0, 3)
    settled = jnp.concatenate([settled, jnp.zeros((NY, NZ - GROUPS, 2, LANES), jnp.float32)], axis=1)

    by_block = pseudo_grad[0].reshape(ROW_TILES, 8, GROUPS, NY, LANES)

    def block_class(index):
        taken = lax.dynamic_index_in_dim(by_block, index % NY, 3, keepdims=False)
        return taken.transpose(0, 2, 1, 3).reshape(ROW_TILES * GROUPS, 8, LANES)

    over_y, settled = summed_around(block_class, settled.reshape(NY, 4, 8, LANES), "y", NY)
    settled = settled.reshape(NY, NZ, 2, LANES).transpose(1, 0, 2, 3).reshape(NZ, 8, LANES)
    settled = rolled(settled, -GROUPS * z).reshape(4, 4, 8, LANES).transpose(1, 0, 2, 3)
    classes = over_y.reshape(GROUPS, 4, 4, 8, LANES).transpose(2, 1, 0, 3, 4)
    windows = summed_in_window(classes.reshape(4, 4 * GROUPS, 8, LANES), settled, "z", NZ)
    far = [[4 * h + l for h in range(4)] for l in range(4)]
    windows = lax.all_to_all(windows, "z", 0, 0, tiled=True, axis_index_groups=far)
    chosen = (send_index[:, None] == jnp.arange(256, dtype=jnp.int32)[None, :]).astype(jnp.bfloat16)

    outgoing = pl.pallas_call(
        outgoing_kernel,
        out_shape=jax.ShapeDtypeStruct((ROWS_SENT * islands, LANES), jnp.float32),
        in_specs=[IN_VMEM] * 2,
        out_specs=IN_VMEM,
        compiler_params=pltpu.CompilerParams(vmem_limit_bytes=6 << 20),
    )(windows, chosen)
    arrived = exchanged(outgoing.reshape(-1, 1, LANES), ISLAND).reshape(-1, LANES)
    over_islands = pl.pallas_call(
        part_kernel,
        out_shape=jax.ShapeDtypeStruct((8, LANES), jnp.float32),
        in_specs=[IN_VMEM],
        out_specs=IN_VMEM,
        compiler_params=pltpu.CompilerParams(vmem_limit_bytes=4 << 20),
    )(arrived)
    eight = exchanged(over_islands.reshape(lax.axis_size(TENSOR), -1, LANES), TENSOR).reshape(-1, LANES)

    flat = jnp.arange(2 * PER_ROW, dtype=jnp.int32)
    even, block = flat // PER_ROW, flat % PER_ROW
    mine = rows_of(arrived, (((GROUPS * z + block // NY) % NZ) * NY + block % NY) * ROWS_SENT + 9 + even).reshape(2, -1)
    gradient_pages = rows_of(arrived, source * ROWS_SENT + 1 + slot)
    settled_pages = rows_of(arrived, source * ROWS_SENT + 5 + slot)
    new_master, new_momentum, packed = pl.pallas_call(
        final_kernel,
        out_shape=(
            jax.ShapeDtypeStruct(mine.shape, jnp.float32),
            jax.ShapeDtypeStruct(mine.shape, jnp.float32),
            jax.ShapeDtypeStruct(gradient_pages.shape, jnp.bfloat16),
        ),
        in_specs=[pl.BlockSpec(memory_space=pltpu.SMEM)] + [IN_VMEM] * 6,
        out_specs=(IN_VMEM, IN_VMEM, IN_VMEM),
        compiler_params=pltpu.CompilerParams(vmem_limit_bytes=4 << 20),
    )(own_length, eight, mine, outer_params, momentum, gradient_pages, settled_pages)
    return (new_master, new_momentum, packed[None])


def part_kernel(arrived, out):
    parts = arrived[pl.ds(0, NZ * NY, stride=ROWS_SENT), :]
    out[...] = jnp.broadcast_to(jnp.sum(parts, axis=0, keepdims=True), out.shape)


def final_kernel(length, eight, mine, params, momentum, gradient_pages, settled_pages, master_out, momentum_out, pages_out):
    square_sum = jnp.sum(eight[...], axis=0, keepdims=True) / (eight.shape[0] // TENSOR_SIZE)
    scale = 1.0 / jnp.sqrt(square_sum / ENTRIES + epsilon)
    normed = mine[...] * scale[:, :1]
    new_momentum = decay_rate * momentum[...] + normed
    momentum_out[...] = new_momentum
    master_out[...] = params[...] - outer_rate * (normed + decay_rate * new_momentum)
    pages = settled_pages[...] - (outer_rate * (1.0 + decay_rate)) * (gradient_pages[...] * scale)
    place = lax.broadcasted_iota(jnp.int32, pages.shape, 0)
    pages_out[...] = jnp.where(place < length[0], pages, 0.0).astype(jnp.bfloat16)


def solution(mesh):
    split = Mesh(mesh.devices.reshape(NZ, NY, 4, 2), ("z", "y", "x", "core"))
    return jax.shard_map(
        body,
        mesh=split,
        in_specs=(P(ISLAND, None, TENSOR), P(ISLAND, TENSOR), P(ISLAND, TENSOR), P(), P()),
        out_specs=(P(ISLAND, TENSOR), P(ISLAND, TENSOR), P(ISLAND, None, TENSOR)),
        check_vma=False,
    )
```
